256 devices in a mesh: wide: 64 (over z_hi, y, x, core), narrow: 4 (over z_lo).
Axes of the slice: x: 4, y: 4, z: 8 (z_hi: 2, z_lo: 4; z = z_hi * 4 + z_lo), core: 2. Of those that a mesh axis runs over, the one named last changes fastest.
Arguments:
- state: float32 [2, 67108864], P(None, ('wide', 'narrow')), may hold values from -6 to 6
- gates: float32 [8, 2, 64, 64], replicated, may hold values from -0.5 to 0.5
- roster: int32 [10], replicated, may hold values from 0 to 7
Outputs:
- final_state: float32 [2, 67108864], P(None, ('wide', 'narrow'))
The draws below stay inside these ranges and needn't reach their ends.
All inputs are finite; a program needn't handle non-finite values.
Results may differ from the reference program's by a relative error of at most 0.00012.
Values sent between devices are 32-bit elements; how exact they have to be, the bound alone decides.
No kernel may reach another device: no remote copies, remote signals or barrier semaphores. Data moves between devices by JAX's collectives and lax.ppermute only.
A program may use at most 64 MiB of HBM per device.

```python
import jax
import jax.numpy as jnp
from jax import lax

LOCAL = 262144
GATE = 64
BANK = 8
ROUNDS = 2
LAYERS = 10
AMPS = 67108864
N_WIDE = 64
N_NARROW = 4


def with_ends(drawn, key, least, high):
    spot = [jax.random.randint(jax.random.fold_in(key, axis), (), 0, length) for axis, length in enumerate(drawn.shape)]
    longest = drawn.shape.index(max(drawn.shape))
    neighbour = spot[:longest] + [(spot[longest] + 1) % drawn.shape[longest]] + spot[longest + 1:]
    return drawn.at[tuple(spot)].set(least).at[tuple(neighbour)].set(high)


def shard_levels(key, dims, cuts, low, largest):
    def one(dim, blocks):
        heights = jax.random.uniform(jax.random.fold_in(jax.random.fold_in(key, 6), dim), (blocks,), jnp.float32, low / len(cuts), largest / len(cuts))
        return jnp.repeat(jnp.exp(heights), dims[dim] // blocks).reshape((-1,) + (1,) * (len(dims) - dim - 1))

    factor_of = one(*cuts[0])
    for cut in cuts[1:]:
        factor_of = factor_of * one(*cut)
    return factor_of


def normal_values(rng, shape, spread, limit, shards=(), dtype=jnp.bfloat16):
    result = jax.random.normal(rng, shape, jnp.float32) * spread
    if len(shards) > 0:
        result = shard_levels(rng, shape, shards, -0.22, 0.18) * result
    return jnp.clip(result, min=-limit, max=limit).astype(dtype)


def setup_inputs(seed: int = 0) -> dict:
    arg_keys = jax.random.split(jax.random.key(seed), 4)
    state = normal_values(arg_keys[0], (2, AMPS), 1.0, 6.0, ((1, 256),), jnp.float32)
    gates = normal_values(arg_keys[1], (BANK, 2, GATE, GATE), (2 * GATE) ** -0.5, 0.5, (), jnp.float32)
    roster = with_ends(jax.random.randint(arg_keys[2], (LAYERS,), 0, BANK), jax.random.fold_in(arg_keys[2], 1), 0, BANK - 1).astype(jnp.int32)
    return dict(state=state, gates=gates, roster=roster)


def block_of(gate):
    real_part = gate[0]
    imag_part = gate[1]
    top = jnp.stack([real_part, -imag_part])
    bottom = jnp.stack([imag_part, real_part])
    return jnp.stack([top, bottom])


def apply_gate(amps, gate, low):
    view = amps.reshape(2, -1, 64, low)
    block = block_of(gate)
    out = jnp.einsum("cagb,dchg->dahb", view, block, precision=lax.Precision.HIGHEST)
    return out.reshape(2, -1)


def reference(state, gates, roster):
    top_low = LOCAL // 64
    amps = state
    for rnd in range(ROUNDS):
        k = 5 * rnd
        amps = apply_gate(amps, gates[roster[k]], 128)
        amps = apply_gate(amps, gates[roster[k + 1]], top_low)
        amps = amps.reshape(2, N_WIDE, N_NARROW, N_NARROW, LOCAL // N_NARROW).swapaxes(2, 3).reshape(2, -1)
        amps = apply_gate(amps, gates[roster[k + 2]], top_low)
        amps = amps.reshape(2, N_WIDE, N_NARROW, N_WIDE, LOCAL // N_WIDE).swapaxes(1, 3).reshape(2, -1)
        amps = apply_gate(amps, gates[roster[k + 3]], top_low)
        amps = apply_gate(amps, gates[roster[k + 4]], 128)
    return amps
```

```python
import functools

import jax
import jax.numpy as jnp
from jax import lax
from jax.experimental import pallas as pl
from jax.experimental.pallas import tpu as pltpu
from jax.sharding import PartitionSpec as P

F32 = jnp.float32
BF16 = jnp.bfloat16

HC, HCL, ROT, CH = "h c", "h5 c h4-0", "h3-0 h5-4 c", "c h"


def source_of(order, i):
    if order == HC:
        return ((i & 1) << 6) | (i >> 1)
    if order == HCL:
        return (((i >> 5) & 1) << 6) | ((i >> 6) << 5) | (i & 31)
    if order == ROT:
        return ((i & 1) << 6) | (((i >> 1) & 3) << 4) | (i >> 3)
    return i


def one_hot(order, dim):
    i = lax.broadcasted_iota(jnp.int32, (128, 128), dim)
    j = lax.broadcasted_iota(jnp.int32, (128, 128), 1 - dim)
    return jnp.where(source_of(order, i) == j, 1.0, 0.0).astype(BF16)


def halves(x):
    high = x.astype(BF16)
    return high, (x - high.astype(F32)).astype(BF16)


def dot(a, b):
    return jnp.dot(a, b, preferred_element_type=F32)


def exact(a, b):
    return jnp.dot(a, b, preferred_element_type=F32, precision=lax.Precision.HIGHEST)


def compose(second, first):
    (r2, i2), (r1, i1) = second, first
    return exact(r2, r1) - exact(i2, i1), exact(r2, i1) + exact(i2, r1)


def operand(gate, order_out, order_in):
    real, imag = gate
    columns = one_hot(order_in, 1)
    rows = one_hot(order_out, 0)
    left = halves(jnp.concatenate([real, imag], 0))
    right = halves(jnp.concatenate([-imag, real], 0))
    parts = [
        dot(rows, (dot(a, columns[:64]) + dot(b, columns[64:])).astype(BF16)).astype(BF16)
        for a, b in zip(left, right)
    ]
    return jnp.concatenate([parts[0], parts[0], parts[1]], 1)


def apply(w, x):
    high, low = halves(x)
    return dot(w, jnp.concatenate([high, low, high], 0))


def swap_lanes(blocks):
    lane = lax.broadcasted_iota(jnp.int32, blocks[0].shape, 1)
    out = list(blocks)
    for bit, width in ((2, 64), (1, 32)):
        upper = (lane & width) != 0
        for i in range(4):
            if i & bit:
                continue
            a, b = out[i], out[i | bit]
            if width == 64:
                a_moved = pltpu.roll(a, 64, 1)
                b_moved = pltpu.roll(b, 64, 1)
            else:
                a_moved = pltpu.roll(a, 96, 1)
                b_moved = pltpu.roll(b, 32, 1)
            out[i] = jnp.where(upper, b_moved, a)
            out[i | bit] = jnp.where(upper, b, a_moved)
    return out


def gate_at(gates_ref, roster_ref, k):
    return gates_ref[roster_ref[k], 0], gates_ref[roster_ref[k], 1]


def first_kernel(roster_ref, gates_ref, x_ref, out_ref, mid_ref):
    w0 = operand(gate_at(gates_ref, roster_ref, 0), HCL, HC)
    w1 = operand(gate_at(gates_ref, roster_ref, 1), HC, HC)

    def lower(i, carry):
        base = i * 512
        x = jnp.concatenate([x_ref[pl.ds(base + 128 * j, 128), :] for j in range(4)], 1)
        y = apply(w0, x)
        for j in range(4):
            mid_ref[pl.ds(base + 128 * j, 128), :] = y[:, 128 * j:128 * (j + 1)]
        return carry

    lax.fori_loop(0, 8, lower, 0)

    def upper(i, carry):
        base = i * 4
        x = jnp.concatenate([mid_ref[pl.ds(base + j, 128, stride=32), :] for j in range(4)], 1)
        y = apply(w1, x)
        for j in range(4):
            part = y[:, 128 * j:128 * (j + 1)]
            moved = swap_lanes([part[32 * q:32 * (q + 1)] for q in range(4)])
            for p in range(4):
                out_ref[pl.ds(1024 * p + base + j, 32, stride=32), :] = moved[p]
        return carry

    lax.fori_loop(0, 8, upper, 0)


def prepare_kernel(roster_ref, gates_ref, w3_ref, wk_ref, w6_ref, w7_ref, wh_ref, w9_ref):
    gate = functools.partial(gate_at, gates_ref, roster_ref)
    w3_ref[...] = operand(gate(3), HC, HC)
    wk_ref[...] = operand(compose(gate(5), gate(4)), HCL, HCL)
    w6_ref[...] = operand(gate(6), HC, HC)
    w7_ref[...] = operand(gate(7), CH, HC)
    wh_ref[...] = operand(compose(gate(8), gate(2)), HC, ROT)
    w9_ref[...] = operand(gate(9), HC, HCL)


def middle_kernel(w3_ref, wk_ref, w6_ref, w7_ref, x_ref, out_ref, mid_ref):
    w3, wk, w6, w7 = w3_ref[...], wk_ref[...], w6_ref[...], w7_ref[...]

    def third(i, carry):
        base = i * 4
        x = jnp.concatenate([x_ref[pl.ds(base + j, 128, stride=32), :] for j in range(4)], 1)
        y = apply(w3, x)
        for j in range(4):
            mid_ref[pl.ds(base + j, 128, stride=32), :] = y[:, 128 * j:128 * (j + 1)]
        return carry

    lax.fori_loop(0, 8, third, 0)

    def fourth(i, carry):
        base = i * 512
        x = jnp.concatenate([mid_ref[pl.ds(base + 128 * j, 128), :] for j in range(4)], 1)
        y = apply(wk, x)
        for j in range(4):
            mid_ref[pl.ds(base + 128 * j, 128), :] = y[:, 128 * j:128 * (j + 1)]
        return carry

    lax.fori_loop(0, 8, fourth, 0)

    def sixth(i, carry):
        base = i * 4
        x = jnp.concatenate([mid_ref[pl.ds(base + j, 128, stride=32), :] for j in range(4)], 1)
        y = apply(w6, x)
        moved = swap_lanes([y[:, 128 * j:128 * (j + 1)] for j in range(4)])
        x = jnp.concatenate(
            [jnp.concatenate([moved[p][32 * j:32 * (j + 1)] for p in range(4)], 0) for j in range(4)], 1
        )
        y = apply(w7, x)
        for j in range(4):
            for c in range(2):
                out_ref[pl.ds(16 * j + 8 * c + i, 64, stride=64), :] = y[64 * c:64 * (c + 1), 128 * j:128 * (j + 1)]
        return carry

    lax.fori_loop(0, 8, sixth, 0)


def last_kernel(wh_ref, w9_ref, x_ref, out_ref, mid_ref):
    wh, w9 = wh_ref[...], w9_ref[...]

    def eighth(i, carry):
        x = jnp.concatenate([x_ref[pl.ds(1024 * e + i, 128, stride=8), :] for e in range(4)], 1)
        y = apply(wh, x)
        moved = swap_lanes([y[:, 128 * e:128 * (e + 1)] for e in range(4)])
        for p in range(4):
            mid_ref[pl.ds(4 * i + p, 128, stride=32), :] = moved[p]
        return carry

    lax.fori_loop(0, 8, eighth, 0)

    def ninth(i, carry):
        base = i * 512
        x = jnp.concatenate([mid_ref[pl.ds(base + 128 * j, 128), :] for j in range(4)], 1)
        y = apply(w9, x)
        for j in range(4):
            out_ref[pl.ds(base + 128 * j, 128), :] = y[:, 128 * j:128 * (j + 1)]
        return carry

    lax.fori_loop(0, 8, ninth, 0)


ROWS = 4096
WHOLE = pl.BlockSpec(memory_space=pltpu.VMEM)
SCALARS = pl.BlockSpec(memory_space=pltpu.SMEM)
AMPS = jax.ShapeDtypeStruct((ROWS, 128), F32)
OPERAND = jax.ShapeDtypeStruct((128, 384), BF16)
MID = pltpu.VMEM((ROWS, 128), F32)
PARAMS = pltpu.CompilerParams(vmem_limit_bytes=32 * 1024 * 1024)


def exchange(amps, axes, count):
    chunks = amps.reshape(count, ROWS // count, 128)
    return lax.all_to_all(chunks, axes, split_axis=0, concat_axis=0, tiled=True).reshape(ROWS, 128)


def on_device(state, gates, roster):
    rows = state.reshape(2, -1, 128).swapaxes(0, 1).reshape(ROWS, 128)
    amps = pl.pallas_call(
        first_kernel, out_shape=AMPS, in_specs=[SCALARS, WHOLE, WHOLE], out_specs=WHOLE,
        scratch_shapes=[MID], compiler_params=PARAMS, name="first",
    )(roster, gates, rows)
    w3, wk, w6, w7, wh, w9 = pl.pallas_call(
        prepare_kernel, out_shape=[OPERAND] * 6, in_specs=[SCALARS, WHOLE], out_specs=[WHOLE] * 6,
        compiler_params=PARAMS, name="prepare",
    )(roster, gates)
    amps = exchange(amps, ("wide",), lax.axis_size("wide"))
    amps = pl.pallas_call(
        middle_kernel, out_shape=AMPS, in_specs=[WHOLE] * 5, out_specs=WHOLE,
        scratch_shapes=[MID], compiler_params=PARAMS, name="middle",
    )(w3, wk, w6, w7, amps)
    amps = exchange(amps, ("wide", "narrow"), lax.axis_size("wide") * lax.axis_size("narrow"))
    amps = pl.pallas_call(
        last_kernel, out_shape=AMPS, in_specs=[WHOLE] * 3, out_specs=WHOLE,
        scratch_shapes=[MID], compiler_params=PARAMS, name="last",
    )(wh, w9, amps)
    return amps.reshape(-1, 2, 128).swapaxes(0, 1).reshape(2, -1)


def solution(mesh):
    in_specs = (P(None, ("wide", "narrow")), P(), P())
    out_specs = P(None, ("wide", "narrow"))
    return jax.shard_map(
        on_device, mesh=mesh, in_specs=in_specs, out_specs=out_specs, check_vma=False
    )
```

```python
import functools

import jax
import jax.numpy as jnp
from jax import lax
from jax.experimental import pallas as pl
from jax.experimental.pallas import tpu as pltpu
from jax.sharding import PartitionSpec as P

F32 = jnp.float32
BF16 = jnp.bfloat16

HC, HCL, HCM, ROT = "h c", "h5 c h4-0", "h5 c h1-0 h4-2", "h3-0 h5-4 c"


def source_of(order, i):
    if order == HC:
        return ((i & 1) << 6) | (i >> 1)
    if order == HCL:
        return (((i >> 5) & 1) << 6) | ((i >> 6) << 5) | (i & 31)
    if order == HCM:
        return (((i >> 5) & 1) << 6) | ((i >> 6) << 5) | ((i & 7) << 2) | ((i >> 3) & 3)
    return ((i & 1) << 6) | (((i >> 1) & 3) << 4) | (i >> 3)


def one_hot(order, dim):
    i = lax.broadcasted_iota(jnp.int32, (128, 128), dim)
    j = lax.broadcasted_iota(jnp.int32, (128, 128), 1 - dim)
    return jnp.where(source_of(order, i) == j, 1.0, 0.0).astype(BF16)


def halves(x):
    high = x.astype(BF16)
    return high, (x - high.astype(F32)).astype(BF16)


def dot(a, b):
    return jnp.dot(a, b, preferred_element_type=F32)


def exact(a, b):
    return jnp.dot(a, b, preferred_element_type=F32, precision=lax.Precision.HIGHEST)


def compose(second, first):
    (r2, i2), (r1, i1) = second, first
    return exact(r2, r1) - exact(i2, i1), exact(r2, i1) + exact(i2, r1)


def operand(gate, order_out, order_in):
    real, imag = gate
    source = one_hot(order_in, 1)
    target = one_hot(order_out, 0)
    left = halves(jnp.concatenate([real, imag], 0))
    right = halves(jnp.concatenate([-imag, real], 0))
    parts = [
        dot(target, (dot(a, source[:64]) + dot(b, source[64:])).astype(BF16)).astype(BF16)
        for a, b in zip(left, right)
    ]
    return jnp.concatenate([parts[0], parts[0], parts[1]], 1)


def apply(w, x):
    high, low = halves(x)
    return dot(w, jnp.concatenate([high, low, high], 0))


def lane_exchange():
    i = lax.broadcasted_iota(jnp.int32, (512, 512), 0)
    j = lax.broadcasted_iota(jnp.int32, (512, 512), 1)
    moved = (((j >> 5) & 3) << 7) | ((j >> 7) << 5) | (j & 31)
    return jnp.where(i == moved, 1.0, 0.0).astype(BF16)


def exchange_lanes(swap, x):
    high, low = halves(x)
    return dot(high, swap) + dot(low, swap)


def columns(blocks):
    return jnp.concatenate(blocks, 1)


def column(x, j):
    return x[:, 128 * j:128 * (j + 1)]


def unpack(x):
    x = jnp.swapaxes(x, 0, 1)
    return columns([x[j] for j in range(8)])


def pack(blocks):
    return jnp.swapaxes(jnp.stack(blocks, 0), 0, 1)


def contiguous(w, x_ref, out_ref):
    for i in range(8):
        blocks = [x_ref[4 * i + j].reshape(128, 128) for j in range(4)]
        y = apply(w, columns(blocks))
        for j in range(4):
            out_ref[4 * i + j] = column(y, j).reshape(out_ref.shape[1:])


def gate_at(gates_ref, roster_ref, k):
    return gates_ref[roster_ref[k], 0], gates_ref[roster_ref[k], 1]


def first_kernel(roster_ref, gates_ref, x_ref, out_ref, mid_ref):
    w0 = operand(gate_at(gates_ref, roster_ref, 0), HCL, HC)
    w1 = operand(gate_at(gates_ref, roster_ref, 1), HC, HC)
    swap = lane_exchange()
    contiguous(w0, x_ref, mid_ref)
    for g in range(4):
        y = apply(w1, unpack(mid_ref[:, :, 8 * g:8 * (g + 1), :].reshape(128, 8, 128)))
        z = jnp.concatenate(
            [columns([column(y, j)[32 * q:32 * (q + 1)] for q in range(4)]) for j in range(8)], 0
        )
        z = exchange_lanes(swap, z)
        for p in range(4):
            moved = jnp.swapaxes(column(z, p).reshape(8, 32, 128), 0, 1)
            out_ref[32 * p:32 * (p + 1), 8 * g:8 * (g + 1), :] = moved


def prepare_kernel(roster_ref, gates_ref, w3_ref, wk_ref, w6_ref, w7_ref, wh_ref, w9_ref):
    gate = functools.partial(gate_at, gates_ref, roster_ref)
    w3_ref[...] = operand(gate(3), HC, HC)
    wk_ref[...] = operand(compose(gate(5), gate(4)), HCM, HCL)
    w6_ref[...] = operand(gate(6), HC, HC)
    w7_ref[...] = operand(gate(7), HC, HC)
    wh_ref[...] = operand(compose(gate(8), gate(2)), HC, ROT)
    w9_ref[...] = operand(gate(9), HC, HCL)


def middle_kernel(w3_ref, wk_ref, w6_ref, w7_ref, x_ref, out_ref, mid_ref, low_ref, high_ref):
    w3, wk, w6, w7 = w3_ref[...], wk_ref[...], w6_ref[...], w7_ref[...]
    swap = lane_exchange()
    for g in range(4):
        y = apply(w3, unpack(x_ref[:, 8 * g:8 * (g + 1), :]))
        moved = pack([column(y, j) for j in range(8)])
        mid_ref[:, :, 8 * g:8 * (g + 1), :] = moved.reshape(32, 4, 8, 128)
    contiguous(wk, mid_ref, low_ref)
    for q in range(4):
        y = apply(w6, unpack(low_ref[:, :, 8 * q:8 * (q + 1), :].reshape(128, 8, 128)))
        for j in range(8):
            high_ref[q, j] = column(y, j)
    for i in range(8):
        z = exchange_lanes(swap, columns([high_ref[q, i] for q in range(4)]))
        x = columns(
            [jnp.concatenate([column(z, p)[32 * j:32 * (j + 1)] for p in range(4)], 0) for j in range(4)]
        )
        y = apply(w7, x)
        for j in range(4):
            mid_ref[8 * j + i] = column(y, j).reshape(4, 32, 128)
    for j in range(4):
        moved = pack([mid_ref[8 * j + i].reshape(128, 128) for i in range(8)])
        out_ref[:, j] = moved.reshape(64, 2, 8, 128)


def last_kernel(wh_ref, w9_ref, x_ref, out_ref, mid_ref, high_ref):
    wh, w9 = wh_ref[...], w9_ref[...]
    swap = lane_exchange()
    for e in range(4):
        y = apply(wh, unpack(x_ref[e]))
        for j in range(8):
            high_ref[e, j] = column(y, j)
    for g in range(4):
        blocks = []
        for i in range(2):
            z = exchange_lanes(swap, columns([high_ref[e, 2 * g + i] for e in range(4)]))
            blocks += [column(z, p) for p in range(4)]
        mid_ref[:, :, 8 * g:8 * (g + 1), :] = pack(blocks).reshape(32, 4, 8, 128)
    contiguous(w9, mid_ref, out_ref)


WHOLE = pl.BlockSpec(memory_space=pltpu.VMEM)
SCALARS = pl.BlockSpec(memory_space=pltpu.SMEM)
OPERAND = jax.ShapeDtypeStruct((128, 384), BF16)
MID = pltpu.VMEM((32, 4, 32, 128), F32)
HIGH = pltpu.VMEM((4, 8, 128, 128), F32)
PARAMS = pltpu.CompilerParams(vmem_limit_bytes=32 * 1024 * 1024)


def amps_like(*shape):
    return jax.ShapeDtypeStruct(shape + (128,), F32)


def exchange(amps, axes):
    count = lax.axis_size(axes)
    chunks = amps.reshape(count, -1, 128)
    return lax.all_to_all(chunks, axes, split_axis=0, concat_axis=0, tiled=True)


def on_device(state, gates, roster):
    rows = state.reshape(2, -1, 128).swapaxes(0, 1).reshape(32, 128, 128)
    amps = pl.pallas_call(
        first_kernel, out_shape=amps_like(128, 32), in_specs=[SCALARS, WHOLE, WHOLE], out_specs=WHOLE,
        scratch_shapes=[MID], compiler_params=PARAMS, name="first",
    )(roster, gates, rows)
    w3, wk, w6, w7, wh, w9 = pl.pallas_call(
        prepare_kernel, out_shape=[OPERAND] * 6, in_specs=[SCALARS, WHOLE], out_specs=[WHOLE] * 6,
        compiler_params=PARAMS, name="prepare",
    )(roster, gates)
    amps = exchange(amps, ("wide",)).reshape(128, 32, 128)
    amps = pl.pallas_call(
        middle_kernel, out_shape=amps_like(64, 4, 2, 8), in_specs=[WHOLE] * 5, out_specs=WHOLE,
        scratch_shapes=[MID, MID, HIGH], compiler_params=PARAMS, name="middle",
    )(w3, wk, w6, w7, amps)
    amps = exchange(amps, ("wide", "narrow")).reshape(4, 128, 8, 128)
    amps = pl.pallas_call(
        last_kernel, out_shape=amps_like(32, 128), in_specs=[WHOLE] * 3, out_specs=WHOLE,
        scratch_shapes=[MID, HIGH], compiler_params=PARAMS, name="last",
    )(wh, w9, amps)
    return amps.reshape(-1, 2, 128).swapaxes(0, 1).reshape(2, -1)


def solution(mesh):
    in_specs = (P(None, ("wide", "narrow")), P(), P())
    out_specs = P(None, ("wide", "narrow"))
    return jax.shard_map(
        on_device, mesh=mesh, in_specs=in_specs, out_specs=out_specs, check_vma=False
    )
```

```python
import functools

import jax
import jax.numpy as jnp
from jax import lax
from jax.experimental import pallas as pl
from jax.experimental.pallas import tpu as pltpu
from jax.sharding import PartitionSpec as P

F32 = jnp.float32
BF16 = jnp.bfloat16

HC, HCL, HCM, ROT = "h c", "h5 c h4-0", "h5 c h1-0 h4-2", "h3-0 h5-4 c"


def source_of(order, i):
    if order == HC:
        return ((i & 1) << 6) | (i >> 1)
    if order == HCL:
        return (((i >> 5) & 1) << 6) | ((i >> 6) << 5) | (i & 31)
    if order == HCM:
        return (((i >> 5) & 1) << 6) | ((i >> 6) << 5) | ((i & 7) << 2) | ((i >> 3) & 3)
    return ((i & 1) << 6) | (((i >> 1) & 3) << 4) | (i >> 3)


def one_hot(order, dim):
    i = lax.broadcasted_iota(jnp.int32, (128, 128), dim)
    j = lax.broadcasted_iota(jnp.int32, (128, 128), 1 - dim)
    return jnp.where(source_of(order, i) == j, 1.0, 0.0).astype(BF16)


def halves(x):
    high = x.astype(BF16)
    return high, (x - high.astype(F32)).astype(BF16)


def dot(a, b):
    return jnp.dot(a, b, preferred_element_type=F32)


def exact(a, b):
    return jnp.dot(a, b, preferred_element_type=F32, precision=lax.Precision.HIGHEST)


def compose(second, first):
    (r2, i2), (r1, i1) = second, first
    return exact(r2, r1) - exact(i2, i1), exact(r2, i1) + exact(i2, r1)


def operand(gate, order_out, order_in):
    real, imag = gate
    source = one_hot(order_in, 1)
    target = one_hot(order_out, 0)
    left = halves(jnp.concatenate([real, imag], 0))
    right = halves(jnp.concatenate([-imag, real], 0))
    parts = [
        dot(target, (dot(a, source[:64]) + dot(b, source[64:])).astype(BF16)).astype(BF16)
        for a, b in zip(left, right)
    ]
    return jnp.concatenate([parts[0], parts[0], parts[1]], 1)


def apply(w, x):
    high, low = halves(x)
    return dot(w, jnp.concatenate([high, low, high], 0))


def lane_exchange():
    i = lax.broadcasted_iota(jnp.int32, (128, 128), 0)
    j = lax.broadcasted_iota(jnp.int32, (128, 128), 1)
    shift, target = i - j, j >> 5
    return jnp.concatenate([
        columns([
            jnp.where((shift == 32 * (p - q)) & (target == q), 1.0, 0.0).astype(BF16) for p in range(4)
        ]) for q in range(4)
    ], 0)


def exchange_lanes(swap, x):
    high, low = halves(x)
    return dot(high, swap) + dot(low, swap)


def columns(blocks):
    return jnp.concatenate(blocks, 1)


def column(x, j):
    return x[:, 128 * j:128 * (j + 1)]


def unpack(x):
    x = jnp.swapaxes(x, 0, 1)
    return columns([x[j] for j in range(8)])


def pack(blocks):
    return jnp.swapaxes(jnp.stack(blocks, 0), 0, 1)


def nothing(i):
    pass


def contiguous(w, x_ref, out_ref, before=nothing, after=nothing):
    for i in range(8):
        before(i)
        blocks = [x_ref[4 * i + j].reshape(128, 128) for j in range(4)]
        y = apply(w, columns(blocks))
        for j in range(4):
            out_ref[4 * i + j] = column(y, j).reshape(out_ref.shape[1:])
        after(i)


def gate_at(gates_ref, roster_ref, k):
    return gates_ref[roster_ref[k], 0], gates_ref[roster_ref[k], 1]


def first_kernel(roster_hbm, gates_hbm, x_hbm, out_hbm, roster_ref, gates_ref, x_ref, mid_ref, out_ref, sems):
    roster_copy = pltpu.make_async_copy(roster_hbm, roster_ref, sems.at[0])
    gates_copy = pltpu.make_async_copy(gates_hbm, gates_ref, sems.at[1])
    x_copies = [
        pltpu.make_async_copy(x_hbm.at[4 * i:4 * i + 4], x_ref.at[4 * i:4 * i + 4], sems.at[2 + i])
        for i in range(8)
    ]
    out_copies = [
        pltpu.make_async_copy(out_ref.at[g], out_hbm.at[:, 8 * g:8 * g + 8], sems.at[10 + g]) for g in range(4)
    ]
    for copy in [roster_copy, gates_copy] + x_copies:
        copy.start()
    swap = lane_exchange()
    roster_copy.wait()
    gates_copy.wait()
    w0 = operand(gate_at(gates_ref, roster_ref, 0), HCL, HC)
    w1 = operand(gate_at(gates_ref, roster_ref, 1), HC, HC)
    contiguous(w0, x_ref, mid_ref, before=lambda i: x_copies[i].wait())
    for g in range(4):
        y = apply(w1, unpack(mid_ref[:, :, 8 * g:8 * (g + 1), :].reshape(128, 8, 128)))
        z = jnp.concatenate(
            [columns([column(y, j)[32 * q:32 * (q + 1)] for q in range(4)]) for j in range(8)], 0
        )
        z = exchange_lanes(swap, z)
        for p in range(4):
            moved = jnp.swapaxes(column(z, p).reshape(8, 32, 128), 0, 1)
            out_ref[g, 32 * p:32 * (p + 1)] = moved
        out_copies[g].start()
    for copy in out_copies:
        copy.wait()


def prepare_kernel(roster_ref, gates_ref, w3_ref, wk_ref, w6_ref, w7_ref, wh_ref, w9_ref, swap_ref):
    swap_ref[...] = lane_exchange()
    gate = functools.partial(gate_at, gates_ref, roster_ref)
    w3_ref[...] = operand(gate(3), HC, HC)
    wk_ref[...] = operand(compose(gate(5), gate(4)), HCM, HCL)
    w6_ref[...] = operand(gate(6), HC, HC)
    w7_ref[...] = operand(gate(7), HC, HC)
    wh_ref[...] = operand(compose(gate(8), gate(2)), HC, ROT)
    w9_ref[...] = operand(gate(9), HC, HCL)


def middle_kernel(w3_ref, wk_ref, w6_ref, w7_ref, swap_ref, x_ref, out_ref, mid_ref, low_ref, high_ref):
    w3, wk, w6, w7 = w3_ref[...], wk_ref[...], w6_ref[...], w7_ref[...]
    swap = swap_ref[...]
    for g in range(4):
        y = apply(w3, unpack(x_ref[:, 8 * g:8 * (g + 1), :]))
        moved = pack([column(y, j) for j in range(8)])
        mid_ref[:, :, 8 * g:8 * (g + 1), :] = moved.reshape(32, 4, 8, 128)
    contiguous(wk, mid_ref, low_ref)
    for q in range(4):
        y = apply(w6, unpack(low_ref[:, :, 8 * q:8 * (q + 1), :].reshape(128, 8, 128)))
        for j in range(8):
            high_ref[q, j] = column(y, j)
    for i in range(8):
        z = exchange_lanes(swap, columns([high_ref[q, i] for q in range(4)]))
        x = columns(
            [jnp.concatenate([column(z, p)[32 * j:32 * (j + 1)] for p in range(4)], 0) for j in range(4)]
        )
        y = apply(w7, x)
        for j in range(4):
            mid_ref[8 * j + i] = column(y, j).reshape(4, 32, 128)
    for j in range(4):
        moved = pack([mid_ref[8 * j + i].reshape(128, 128) for i in range(8)])
        out_ref[:, j] = moved.reshape(64, 2, 8, 128)


def last_kernel(wh_ref, w9_ref, swap_ref, x_ref, out_hbm, mid_ref, high_ref, out_ref, sems):
    wh, w9 = wh_ref[...], w9_ref[...]
    swap = swap_ref[...]
    out_copies = [
        pltpu.make_async_copy(out_ref.at[4 * i:4 * i + 4], out_hbm.at[4 * i:4 * i + 4], sems.at[i])
        for i in range(8)
    ]
    for e in range(4):
        y = apply(wh, unpack(x_ref[e]))
        for j in range(8):
            high_ref[e, j] = column(y, j)
    for g in range(4):
        blocks = []
        for i in range(2):
            z = exchange_lanes(swap, columns([high_ref[e, 2 * g + i] for e in range(4)]))
            blocks += [column(z, p) for p in range(4)]
        mid_ref[:, :, 8 * g:8 * (g + 1), :] = pack(blocks).reshape(32, 4, 8, 128)
    contiguous(w9, mid_ref, out_ref, after=lambda i: out_copies[i].start())
    for copy in out_copies:
        copy.wait()


WHOLE = pl.BlockSpec(memory_space=pltpu.VMEM)
SCALARS = pl.BlockSpec(memory_space=pltpu.SMEM)
IN_HBM = pl.BlockSpec(memory_space=pltpu.HBM)
OPERAND = jax.ShapeDtypeStruct((128, 384), BF16)
MID = pltpu.VMEM((32, 4, 32, 128), F32)
SWAP = jax.ShapeDtypeStruct((512, 512), BF16)
FLAT = pltpu.VMEM((32, 128, 128), F32)
HIGH = pltpu.VMEM((4, 8, 128, 128), F32)
PARAMS = pltpu.CompilerParams(vmem_limit_bytes=16 * 1024 * 1024)
ALL_VMEM = pltpu.CompilerParams(vmem_limit_bytes=63 * 1024 * 1024)


def amps_like(*shape):
    return jax.ShapeDtypeStruct(shape + (128,), F32)


def exchange(amps, axes):
    count = lax.axis_size(axes)
    chunks = amps.reshape(count, -1, 128)
    return lax.all_to_all(chunks, axes, split_axis=0, concat_axis=0, tiled=True)


def on_device(state, gates, roster):
    rows = state.reshape(2, -1, 128).swapaxes(0, 1).reshape(32, 128, 128)
    amps = pl.pallas_call(
        first_kernel, out_shape=amps_like(128, 32), in_specs=[IN_HBM] * 3, out_specs=IN_HBM,
        scratch_shapes=[
            pltpu.SMEM(roster.shape, roster.dtype), pltpu.VMEM(gates.shape, gates.dtype), FLAT, MID,
            pltpu.VMEM((4, 128, 8, 128), F32), pltpu.SemaphoreType.DMA((14,)),
        ],
        compiler_params=ALL_VMEM, name="first",
    )(roster, gates, rows)
    w3, wk, w6, w7, wh, w9, swap = pl.pallas_call(
        prepare_kernel, out_shape=[OPERAND] * 6 + [SWAP], in_specs=[SCALARS, WHOLE], out_specs=[WHOLE] * 7,
        compiler_params=PARAMS, name="prepare",
    )(roster, gates)
    amps = exchange(amps, ("wide",)).reshape(128, 32, 128)
    amps = pl.pallas_call(
        middle_kernel, out_shape=amps_like(64, 4, 2, 8), in_specs=[WHOLE] * 6, out_specs=WHOLE,
        scratch_shapes=[MID, MID, HIGH], compiler_params=PARAMS, name="middle",
    )(w3, wk, w6, w7, swap, amps)
    amps = exchange(amps, ("wide", "narrow")).reshape(4, 128, 8, 128)
    amps = pl.pallas_call(
        last_kernel, out_shape=amps_like(32, 128), in_specs=[WHOLE] * 4, out_specs=IN_HBM,
        scratch_shapes=[MID, HIGH, FLAT, pltpu.SemaphoreType.DMA((8,))], compiler_params=PARAMS, name="last",
    )(wh, w9, swap, amps)
    return amps.reshape(-1, 2, 128).swapaxes(0, 1).reshape(2, -1)


def solution(mesh):
    in_specs = (P(None, ("wide", "narrow")), P(), P())
    out_specs = P(None, ("wide", "narrow"))
    return jax.shard_map(
        on_device, mesh=mesh, in_specs=in_specs, out_specs=out_specs, check_vma=False
    )
```

```python
import functools

import jax
import jax.numpy as jnp
from jax import lax
from jax.experimental import pallas as pl
from jax.experimental.pallas import tpu as pltpu
from jax.sharding import PartitionSpec as P

F32 = jnp.float32
BF16 = jnp.bfloat16

HC, HCL, HCM, ROT = "h c", "h5 c h4-0", "h5 c h1-0 h4-2", "h3-0 h5-4 c"


def source_of(order, i):
    if order == HC:
        return ((i & 1) << 6) | (i >> 1)
    if order == HCL:
        return (((i >> 5) & 1) << 6) | ((i >> 6) << 5) | (i & 31)
    if order == HCM:
        return (((i >> 5) & 1) << 6) | ((i >> 6) << 5) | ((i & 7) << 2) | ((i >> 3) & 3)
    return ((i & 1) << 6) | (((i >> 1) & 3) << 4) | (i >> 3)


def one_hot(order, dim):
    i = lax.broadcasted_iota(jnp.int32, (128, 128), dim)
    j = lax.broadcasted_iota(jnp.int32, (128, 128), 1 - dim)
    return jnp.where(source_of(order, i) == j, 1.0, 0.0).astype(BF16)


def halves(x):
    high = x.astype(BF16)
    return high, (x - high.astype(F32)).astype(BF16)


def dot(a, b):
    return jnp.dot(a, b, preferred_element_type=F32)


def exact(a, b):
    return jnp.dot(a, b, preferred_element_type=F32, precision=lax.Precision.HIGHEST)


def compose(second, first):
    (r2, i2), (r1, i1) = second, first
    return exact(r2, r1) - exact(i2, i1), exact(r2, i1) + exact(i2, r1)


def operand(gate, order_out, order_in):
    real, imag = gate
    source = one_hot(order_in, 1)
    target = one_hot(order_out, 0)
    left = halves(jnp.concatenate([real, imag], 0))
    right = halves(jnp.concatenate([-imag, real], 0))
    parts = [
        dot(target, (dot(a, source[:64]) + dot(b, source[64:])).astype(BF16)).astype(BF16)
        for a, b in zip(left, right)
    ]
    return jnp.concatenate([parts[0], parts[0], parts[1]], 1)


def apply(w, x):
    high, low = halves(x)
    return dot(w, jnp.concatenate([high, low, high], 0))


def lane_exchange():
    i = lax.broadcasted_iota(jnp.int32, (128, 128), 0)
    j = lax.broadcasted_iota(jnp.int32, (128, 128), 1)
    shift, target = i - j, j >> 5
    return jnp.concatenate([
        columns([
            jnp.where((shift == 32 * (p - q)) & (target == q), 1.0, 0.0).astype(BF16) for p in range(4)
        ]) for q in range(4)
    ], 0)


def exchange_lanes(swap, x):
    high, low = halves(x)
    return dot(high, swap) + dot(low, swap)


def columns(blocks):
    return jnp.concatenate(blocks, 1)


def column(x, j):
    return x[:, 128 * j:128 * (j + 1)]


def unpack(x):
    x = jnp.swapaxes(x, 0, 1)
    return columns([x[j] for j in range(8)])


def pack(blocks):
    return jnp.swapaxes(jnp.stack(blocks, 0), 0, 1)


def nothing(i):
    pass


def contiguous(w, x_ref, out_ref, before=nothing, after=nothing):
    for i in range(8):
        before(i)
        blocks = [x_ref[4 * i + j].reshape(128, 128) for j in range(4)]
        y = apply(w, columns(blocks))
        for j in range(4):
            out_ref[4 * i + j] = column(y, j).reshape(out_ref.shape[1:])
        after(i)


def gate_at(gates_ref, roster_ref, k):
    return gates_ref[roster_ref[k], 0], gates_ref[roster_ref[k], 1]


def first_kernel(roster_hbm, gates_hbm, x_hbm, out_hbm, roster_ref, gates_ref, x_ref, mid_ref, out_ref, sems):
    roster_copy = pltpu.make_async_copy(roster_hbm, roster_ref, sems.at[0])
    gates_copy = pltpu.make_async_copy(gates_hbm, gates_ref, sems.at[1])
    x_copies = [
        pltpu.make_async_copy(x_hbm.at[4 * i:4 * i + 4], x_ref.at[4 * i:4 * i + 4], sems.at[2 + i])
        for i in range(8)
    ]
    out_copies = [
        pltpu.make_async_copy(out_ref.at[g], out_hbm.at[:, 8 * g:8 * g + 8], sems.at[10 + g]) for g in range(4)
    ]
    for copy in [roster_copy, gates_copy] + x_copies:
        copy.start()
    swap = lane_exchange()
    roster_copy.wait()
    gates_copy.wait()
    w0 = operand(gate_at(gates_ref, roster_ref, 0), HCL, HC)
    w1 = operand(gate_at(gates_ref, roster_ref, 1), HC, HC)
    contiguous(w0, x_ref, mid_ref, before=lambda i: x_copies[i].wait())
    for g in range(4):
        y = apply(w1, unpack(mid_ref[:, :, 8 * g:8 * (g + 1), :].reshape(128, 8, 128)))
        z = jnp.concatenate(
            [columns([column(y, j)[32 * q:32 * (q + 1)] for q in range(4)]) for j in range(8)], 0
        )
        z = exchange_lanes(swap, z)
        for p in range(4):
            moved = jnp.swapaxes(column(z, p).reshape(8, 32, 128), 0, 1)
            out_ref[g, 32 * p:32 * (p + 1)] = moved
        out_copies[g].start()
    for copy in out_copies:
        copy.wait()


def prepare_kernel(roster_ref, gates_ref, w_ref):
    w_ref[768:] = lane_exchange()
    gate = functools.partial(gate_at, gates_ref, roster_ref)
    w_ref[0:128, :384] = operand(gate(3), HC, HC)
    w_ref[128:256, :384] = operand(compose(gate(5), gate(4)), HCM, HCL)
    w_ref[256:384, :384] = operand(gate(6), HC, HC)
    w_ref[384:512, :384] = operand(gate(7), HC, HC)
    w_ref[512:640, :384] = operand(compose(gate(8), gate(2)), HC, ROT)
    w_ref[640:768, :384] = operand(gate(9), HC, HCL)


def middle_kernel(w_ref, x_ref, out_ref, mid_ref, low_ref, high_ref):
    w3, wk, w6, w7 = [w_ref[128 * k:128 * (k + 1), :384] for k in range(4)]
    swap = w_ref[768:]
    for g in range(4):
        y = apply(w3, unpack(x_ref[:, 8 * g:8 * (g + 1), :]))
        moved = pack([column(y, j) for j in range(8)])
        mid_ref[:, :, 8 * g:8 * (g + 1), :] = moved.reshape(32, 4, 8, 128)
    contiguous(wk, mid_ref, low_ref)
    for q in range(4):
        y = apply(w6, unpack(low_ref[:, :, 8 * q:8 * (q + 1), :].reshape(128, 8, 128)))
        for j in range(8):
            high_ref[q, j] = column(y, j)
    for i in range(8):
        z = exchange_lanes(swap, columns([high_ref[q, i] for q in range(4)]))
        x = columns(
            [jnp.concatenate([column(z, p)[32 * j:32 * (j + 1)] for p in range(4)], 0) for j in range(4)]
        )
        y = apply(w7, x)
        for j in range(4):
            mid_ref[8 * j + i] = column(y, j).reshape(4, 32, 128)
    for j in range(4):
        moved = pack([mid_ref[8 * j + i].reshape(128, 128) for i in range(8)])
        out_ref[:, j] = moved.reshape(64, 2, 8, 128)


def last_kernel(w_ref, x_ref, out_hbm, mid_ref, high_ref, out_ref, sems):
    wh, w9 = w_ref[512:640, :384], w_ref[640:768, :384]
    swap = w_ref[768:]
    out_copies = [
        pltpu.make_async_copy(out_ref.at[4 * i:4 * i + 4], out_hbm.at[4 * i:4 * i + 4], sems.at[i])
        for i in range(8)
    ]
    for e in range(4):
        y = apply(wh, unpack(x_ref[e]))
        for j in range(8):
            high_ref[e, j] = column(y, j)
    for g in range(4):
        blocks = []
        for i in range(2):
            z = exchange_lanes(swap, columns([high_ref[e, 2 * g + i] for e in range(4)]))
            blocks += [column(z, p) for p in range(4)]
        mid_ref[:, :, 8 * g:8 * (g + 1), :] = pack(blocks).reshape(32, 4, 8, 128)
    contiguous(w9, mid_ref, out_ref, after=lambda i: out_copies[i].start())
    for copy in out_copies:
        copy.wait()


WHOLE = pl.BlockSpec(memory_space=pltpu.VMEM)
SCALARS = pl.BlockSpec(memory_space=pltpu.SMEM)
IN_HBM = pl.BlockSpec(memory_space=pltpu.HBM)
OPERANDS = jax.ShapeDtypeStruct((1280, 512), BF16)
MID = pltpu.VMEM((32, 4, 32, 128), F32)
FLAT = pltpu.VMEM((32, 128, 128), F32)
HIGH = pltpu.VMEM((4, 8, 128, 128), F32)
PARAMS = pltpu.CompilerParams(vmem_limit_bytes=16 * 1024 * 1024)
ALL_VMEM = pltpu.CompilerParams(vmem_limit_bytes=63 * 1024 * 1024)


def amps_like(*shape):
    return jax.ShapeDtypeStruct(shape + (128,), F32)


def exchange(amps, axes):
    count = lax.axis_size(axes)
    chunks = amps.reshape(count, -1, 128)
    return lax.all_to_all(chunks, axes, split_axis=0, concat_axis=0, tiled=True)


def on_device(state, gates, roster):
    rows = state.reshape(2, -1, 128).swapaxes(0, 1).reshape(32, 128, 128)
    amps = pl.pallas_call(
        first_kernel, out_shape=amps_like(128, 32), in_specs=[IN_HBM] * 3, out_specs=IN_HBM,
        scratch_shapes=[
            pltpu.SMEM(roster.shape, roster.dtype), pltpu.VMEM(gates.shape, gates.dtype), FLAT, MID,
            pltpu.VMEM((4, 128, 8, 128), F32), pltpu.SemaphoreType.DMA((14,)),
        ],
        compiler_params=ALL_VMEM, name="first",
    )(roster, gates, rows)
    operands = pl.pallas_call(
        prepare_kernel, out_shape=OPERANDS, in_specs=[SCALARS, WHOLE], out_specs=WHOLE,
        compiler_params=PARAMS, name="prepare",
    )(roster, gates)
    amps = exchange(amps, ("wide",)).reshape(128, 32, 128)
    amps = pl.pallas_call(
        middle_kernel, out_shape=amps_like(64, 4, 2, 8), in_specs=[WHOLE] * 2, out_specs=WHOLE,
        scratch_shapes=[MID, MID, HIGH], compiler_params=PARAMS, name="middle",
    )(operands, amps)
    amps = exchange(amps, ("wide", "narrow")).reshape(4, 128, 8, 128)
    amps = pl.pallas_call(
        last_kernel, out_shape=amps_like(32, 128), in_specs=[WHOLE] * 2, out_specs=IN_HBM,
        scratch_shapes=[MID, HIGH, FLAT, pltpu.SemaphoreType.DMA((8,))], compiler_params=PARAMS, name="last",
    )(operands, amps)
    return amps.reshape(-1, 2, 128).swapaxes(0, 1).reshape(2, -1)


def solution(mesh):
    in_specs = (P(None, ("wide", "narrow")), P(), P())
    out_specs = P(None, ("wide", "narrow"))
    return jax.shard_map(
        on_device, mesh=mesh, in_specs=in_specs, out_specs=out_specs, check_vma=False
    )
```

```python
import functools

import jax
import jax.numpy as jnp
from jax import lax
from jax.experimental import pallas as pl
from jax.experimental.pallas import tpu as pltpu
from jax.sharding import PartitionSpec as P

F32 = jnp.float32
BF16 = jnp.bfloat16

HC, HCL, HCM = "h c", "h5 c h4-0", "h5 c h1-0 h4-2"
WIDE, WHOLE_MESH = "h4-1 h5 h0 c", "h1 h3-2 h0 h5-4 c"


def source_of(order, i):
    if order == HC:
        return ((i & 1) << 6) | (i >> 1)
    if order == HCL:
        return (((i >> 5) & 1) << 6) | ((i >> 6) << 5) | (i & 31)
    if order == HCM:
        return (((i >> 5) & 1) << 6) | ((i >> 6) << 5) | ((i & 7) << 2) | ((i >> 3) & 3)
    if order == WIDE:
        return ((i & 1) << 6) | (((i >> 2) & 1) << 5) | (((i >> 3) & 15) << 1) | ((i >> 1) & 1)
    return (
        ((i & 1) << 6) | (((i >> 1) & 3) << 4) | (((i >> 4) & 3) << 2) | ((i >> 6) << 1) | ((i >> 3) & 1)
    )


def one_hot(order, dim):
    i = lax.broadcasted_iota(jnp.int32, (128, 128), dim)
    j = lax.broadcasted_iota(jnp.int32, (128, 128), 1 - dim)
    return jnp.where(source_of(order, i) == j, 1.0, 0.0).astype(BF16)


def halves(x):
    high = x.astype(BF16)
    return high, (x - high.astype(F32)).astype(BF16)


def dot(a, b):
    return jnp.dot(a, b, preferred_element_type=F32)


def exact(a, b):
    return jnp.dot(a, b, preferred_element_type=F32, precision=lax.Precision.HIGHEST)


def compose(second, first):
    (r2, i2), (r1, i1) = second, first
    return exact(r2, r1) - exact(i2, i1), exact(r2, i1) + exact(i2, r1)


def operand(gate, order_out, order_in):
    real, imag = gate
    source = one_hot(order_in, 1)
    target = one_hot(order_out, 0)
    left = halves(jnp.concatenate([real, imag], 0))
    right = halves(jnp.concatenate([-imag, real], 0))
    parts = [
        dot(target, (dot(a, source[:64]) + dot(b, source[64:])).astype(BF16)).astype(BF16)
        for a, b in zip(left, right)
    ]
    return jnp.concatenate([parts[0], parts[0], parts[1]], 1)


def apply(w, x):
    high, low = halves(x)
    return dot(w, jnp.concatenate([high, low, high], 0))


def lane_exchange():
    i = lax.broadcasted_iota(jnp.int32, (128, 128), 0)
    j = lax.broadcasted_iota(jnp.int32, (128, 128), 1)
    shift, target = i - j, j >> 5
    return jnp.concatenate([
        columns([
            jnp.where((shift == 32 * (p - q)) & (target == q), 1.0, 0.0).astype(BF16) for p in range(4)
        ]) for q in range(4)
    ], 0)


def exchange_lanes(swap, x):
    high, low = halves(x)
    return dot(high, swap) + dot(low, swap)


def columns(blocks):
    return jnp.concatenate(blocks, 1)


def column(x, j):
    return x[:, 128 * j:128 * (j + 1)]


def unpack(x):
    x = jnp.swapaxes(x, 0, 1)
    return columns([x[j] for j in range(8)])


def pack(blocks):
    return jnp.swapaxes(jnp.stack(blocks, 0), 0, 1)


def nothing(i):
    pass


def contiguous(w, x_ref, out_ref, before=nothing, after=nothing):
    for i in range(8):
        before(i)
        blocks = [x_ref[4 * i + j].reshape(128, 128) for j in range(4)]
        y = apply(w, columns(blocks))
        for j in range(4):
            out_ref[4 * i + j] = column(y, j).reshape(out_ref.shape[1:])
        after(i)


def gate_at(gates_ref, roster_ref, k):
    return gates_ref[roster_ref[k], 0], gates_ref[roster_ref[k], 1]


def first_kernel(roster_hbm, gates_hbm, x_hbm, out_hbm, roster_ref, gates_ref, x_ref, mid_ref, out_ref, sems):
    roster_copy = pltpu.make_async_copy(roster_hbm, roster_ref, sems.at[0])
    gates_copy = pltpu.make_async_copy(gates_hbm, gates_ref, sems.at[1])
    x_copies = [
        pltpu.make_async_copy(x_hbm.at[4 * i:4 * i + 4], x_ref.at[4 * i:4 * i + 4], sems.at[2 + i])
        for i in range(8)
    ]
    out_copies = [
        pltpu.make_async_copy(out_ref.at[g], out_hbm.at[:, 8 * g:8 * g + 8], sems.at[10 + g]) for g in range(4)
    ]
    for copy in [roster_copy, gates_copy] + x_copies:
        copy.start()
    swap = lane_exchange()
    roster_copy.wait()
    gates_copy.wait()
    w0 = operand(gate_at(gates_ref, roster_ref, 0), HCL, HC)
    w1 = operand(gate_at(gates_ref, roster_ref, 1), HC, HC)
    contiguous(w0, x_ref, mid_ref, before=lambda i: x_copies[i].wait())
    for g in range(4):
        y = apply(w1, unpack(mid_ref[:, :, 8 * g:8 * (g + 1), :].reshape(128, 8, 128)))
        z = jnp.concatenate(
            [columns([column(y, j)[32 * q:32 * (q + 1)] for q in range(4)]) for j in range(8)], 0
        )
        z = exchange_lanes(swap, z)
        for p in range(4):
            moved = jnp.swapaxes(column(z, p).reshape(8, 32, 128), 0, 1)
            out_ref[g, 32 * p:32 * (p + 1)] = moved
        out_copies[g].start()
    for copy in out_copies:
        copy.wait()


def prepare_kernel(roster_ref, gates_ref, w_ref):
    w_ref[768:] = lane_exchange()
    gate = functools.partial(gate_at, gates_ref, roster_ref)
    w_ref[0:128, :384] = operand(gate(3), HC, WIDE)
    w_ref[128:256, :384] = operand(compose(gate(5), gate(4)), HCM, HCL)
    w_ref[256:384, :384] = operand(gate(6), HC, HC)
    w_ref[384:512, :384] = operand(gate(7), HC, HC)
    w_ref[512:640, :384] = operand(compose(gate(8), gate(2)), HC, WHOLE_MESH)
    w_ref[640:768, :384] = operand(gate(9), HC, HCL)


def middle_kernel(w_ref, x_ref, out_ref, mid_ref, low_ref, high_ref):
    w3, wk, w6, w7 = [w_ref[128 * k:128 * (k + 1), :384] for k in range(4)]
    swap = w_ref[768:]
    for g in range(4):
        y = apply(w3, unpack(x_ref[:, 8 * g:8 * (g + 1), :]))
        moved = pack([column(y, j) for j in range(8)])
        mid_ref[:, :, 8 * g:8 * (g + 1), :] = moved.reshape(32, 4, 8, 128)
    contiguous(wk, mid_ref, low_ref)
    for q in range(4):
        y = apply(w6, unpack(low_ref[:, :, 8 * q:8 * (q + 1), :].reshape(128, 8, 128)))
        for j in range(8):
            high_ref[q, j] = column(y, j)
    for i in range(8):
        z = exchange_lanes(swap, columns([high_ref[q, i] for q in range(4)]))
        x = columns(
            [jnp.concatenate([column(z, p)[32 * j:32 * (j + 1)] for p in range(4)], 0) for j in range(4)]
        )
        y = apply(w7, x)
        for j in range(4):
            mid_ref[8 * j + i] = column(y, j).reshape(4, 32, 128)
    for j in range(4):
        moved = pack([mid_ref[8 * j + i].reshape(128, 128) for i in range(8)])
        out_ref[:, j] = moved.reshape(64, 2, 8, 128)


def last_kernel(w_ref, x_ref, out_hbm, mid_ref, high_ref, out_ref, sems):
    wh, w9 = w_ref[512:640, :384], w_ref[640:768, :384]
    swap = w_ref[768:]
    out_copies = [
        pltpu.make_async_copy(out_ref.at[4 * i:4 * i + 4], out_hbm.at[4 * i:4 * i + 4], sems.at[i])
        for i in range(8)
    ]
    for e in range(4):
        y = apply(wh, unpack(jnp.concatenate([x_ref[0, e], x_ref[1, e]], 0)))
        for j in range(8):
            high_ref[e, j] = column(y, j)
    for g in range(4):
        blocks = []
        for i in range(2):
            z = exchange_lanes(swap, columns([high_ref[e, 2 * g + i] for e in range(4)]))
            blocks += [column(z, p) for p in range(4)]
        mid_ref[:, :, 8 * g:8 * (g + 1), :] = pack(blocks).reshape(32, 4, 8, 128)
    contiguous(w9, mid_ref, out_ref, after=lambda i: out_copies[i].start())
    for copy in out_copies:
        copy.wait()


WHOLE = pl.BlockSpec(memory_space=pltpu.VMEM)
SCALARS = pl.BlockSpec(memory_space=pltpu.SMEM)
IN_HBM = pl.BlockSpec(memory_space=pltpu.HBM)
OPERANDS = jax.ShapeDtypeStruct((1280, 512), BF16)
MID = pltpu.VMEM((32, 4, 32, 128), F32)
FLAT = pltpu.VMEM((32, 128, 128), F32)
HIGH = pltpu.VMEM((4, 8, 128, 128), F32)
PARAMS = pltpu.CompilerParams(vmem_limit_bytes=16 * 1024 * 1024)
ALL_VMEM = pltpu.CompilerParams(vmem_limit_bytes=63 * 1024 * 1024)


def amps_like(*shape):
    return jax.ShapeDtypeStruct(shape + (128,), F32)


def exchange(amps, axes):
    count = lax.axis_size(axes)
    chunks = amps.reshape(count, -1, 128)
    return lax.all_to_all(chunks, axes, split_axis=0, concat_axis=0, tiled=True)


def on_device(state, gates, roster):
    rows = state.reshape(2, -1, 128).swapaxes(0, 1).reshape(32, 128, 128)
    amps = pl.pallas_call(
        first_kernel, out_shape=amps_like(128, 32), in_specs=[IN_HBM] * 3, out_specs=IN_HBM,
        scratch_shapes=[
            pltpu.SMEM(roster.shape, roster.dtype), pltpu.VMEM(gates.shape, gates.dtype), FLAT, MID,
            pltpu.VMEM((4, 128, 8, 128), F32), pltpu.SemaphoreType.DMA((14,)),
        ],
        compiler_params=ALL_VMEM, name="first",
    )(roster, gates, rows)
    operands = pl.pallas_call(
        prepare_kernel, out_shape=OPERANDS, in_specs=[SCALARS, WHOLE], out_specs=WHOLE,
        compiler_params=PARAMS, name="prepare",
    )(roster, gates)
    amps = exchange(amps, ("flat", "far", "core")).reshape(128, 32, 128)
    amps = pl.pallas_call(
        middle_kernel, out_shape=amps_like(64, 4, 2, 8), in_specs=[WHOLE] * 2, out_specs=WHOLE,
        scratch_shapes=[MID, MID, HIGH], compiler_params=PARAMS, name="middle",
    )(operands, amps)
    amps = exchange(amps, ("far", "flat", "core", "near")).reshape(2, 4, 64, 8, 128)
    amps = pl.pallas_call(
        last_kernel, out_shape=amps_like(32, 128), in_specs=[WHOLE] * 2, out_specs=IN_HBM,
        scratch_shapes=[MID, HIGH, FLAT, pltpu.SemaphoreType.DMA((8,))], compiler_params=PARAMS, name="last",
    )(operands, amps)
    return amps.reshape(-1, 2, 128).swapaxes(0, 1).reshape(2, -1)


def solution(mesh):
    near = mesh.shape["narrow"]
    flat = mesh.devices.size // near // 4
    cut = jax.sharding.Mesh(mesh.devices.reshape(2, flat, 2, near), ("far", "flat", "core", "near"))
    spec = P(None, ("far", "flat", "core", "near"))
    return jax.shard_map(
        on_device, mesh=cut, in_specs=(spec, P(), P()), out_specs=spec, check_vma=False
    )
```

```python
import functools

import jax
import jax.numpy as jnp
from jax import lax
from jax.experimental import pallas as pl
from jax.experimental.pallas import tpu as pltpu
from jax.sharding import PartitionSpec as P

F32 = jnp.float32
BF16 = jnp.bfloat16

HC, HCL, HCM, ROT = "h c", "h5 c h4-0", "h5 c h1-0 h4-2", "h3-0 h5-4 c"


def source_of(order, i):
    if order == HC:
        return ((i & 1) << 6) | (i >> 1)
    if order == HCL:
        return (((i >> 5) & 1) << 6) | ((i >> 6) << 5) | (i & 31)
    if order == HCM:
        return (((i >> 5) & 1) << 6) | ((i >> 6) << 5) | ((i & 7) << 2) | ((i >> 3) & 3)
    return ((i & 1) << 6) | (((i >> 1) & 3) << 4) | (i >> 3)


def one_hot(order, dim):
    i = lax.broadcasted_iota(jnp.int32, (128, 128), dim)
    j = lax.broadcasted_iota(jnp.int32, (128, 128), 1 - dim)
    return jnp.where(source_of(order, i) == j, 1.0, 0.0).astype(BF16)


def halves(x):
    high = x.astype(BF16)
    return high, (x - high.astype(F32)).astype(BF16)


def dot(a, b):
    return jnp.dot(a, b, preferred_element_type=F32)


def exact(a, b):
    return jnp.dot(a, b, preferred_element_type=F32, precision=lax.Precision.HIGHEST)


def compose(second, first):
    (r2, i2), (r1, i1) = second, first
    return exact(r2, r1) - exact(i2, i1), exact(r2, i1) + exact(i2, r1)


def operand(gate, order_out, order_in):
    real, imag = gate
    source = one_hot(order_in, 1)
    target = one_hot(order_out, 0)
    left = halves(jnp.concatenate([real, imag], 0))
    right = halves(jnp.concatenate([-imag, real], 0))
    parts = [
        dot(target, (dot(a, source[:64]) + dot(b, source[64:])).astype(BF16)).astype(BF16)
        for a, b in zip(left, right)
    ]
    return jnp.concatenate([parts[0], parts[0], parts[1]], 1)


def apply(w, x):
    high, low = halves(x)
    return dot(w, jnp.concatenate([high, low, high], 0))


def lane_exchange():
    i = lax.broadcasted_iota(jnp.int32, (128, 128), 0)
    j = lax.broadcasted_iota(jnp.int32, (128, 128), 1)
    shift, target = i - j, j >> 5
    return jnp.concatenate([
        columns([
            jnp.where((shift == 32 * (p - q)) & (target == q), 1.0, 0.0).astype(BF16) for p in range(4)
        ]) for q in range(4)
    ], 0)


def exchange_lanes(swap, x):
    high, low = halves(x)
    return dot(high, swap) + dot(low, swap)


def columns(blocks):
    return jnp.concatenate(blocks, 1)


def column(x, j):
    return x[:, 128 * j:128 * (j + 1)]


def unpack(x):
    x = jnp.swapaxes(x, 0, 1)
    return columns([x[j] for j in range(8)])


def pack(blocks):
    return jnp.swapaxes(jnp.stack(blocks, 0), 0, 1)


def nothing(i):
    pass


def contiguous(w, x_ref, out_ref, before=nothing, after=nothing):
    for i in range(8):
        before(i)
        blocks = [x_ref[4 * i + j].reshape(128, 128) for j in range(4)]
        y = apply(w, columns(blocks))
        for j in range(4):
            out_ref[4 * i + j] = column(y, j).reshape(out_ref.shape[1:])
        after(i)


def gate_at(gates_ref, roster_ref, k):
    return gates_ref[roster_ref[k], 0], gates_ref[roster_ref[k], 1]


def first_kernel(roster_hbm, gates_hbm, x_hbm, out_hbm, roster_ref, gates_ref, x_ref, mid_ref, out_ref, sems):
    roster_copy = pltpu.make_async_copy(roster_hbm, roster_ref, sems.at[0])
    gates_copy = pltpu.make_async_copy(gates_hbm, gates_ref, sems.at[1])
    x_copies = [
        pltpu.make_async_copy(x_hbm.at[4 * i:4 * i + 4], x_ref.at[4 * i:4 * i + 4], sems.at[2 + i])
        for i in range(8)
    ]
    out_copies = [
        pltpu.make_async_copy(out_ref.at[g], out_hbm.at[:, 8 * g:8 * g + 8], sems.at[10 + g]) for g in range(4)
    ]
    for copy in [roster_copy, gates_copy] + x_copies:
        copy.start()
    swap = lane_exchange()
    roster_copy.wait()
    gates_copy.wait()
    w0 = operand(gate_at(gates_ref, roster_ref, 0), HCL, HC)
    w1 = operand(gate_at(gates_ref, roster_ref, 1), HC, HC)
    contiguous(w0, x_ref, mid_ref, before=lambda i: x_copies[i].wait())
    for g in range(4):
        y = apply(w1, unpack(mid_ref[:, :, 8 * g:8 * (g + 1), :].reshape(128, 8, 128)))
        z = jnp.concatenate(
            [columns([column(y, j)[32 * q:32 * (q + 1)] for q in range(4)]) for j in range(8)], 0
        )
        z = exchange_lanes(swap, z)
        for p in range(4):
            moved = jnp.swapaxes(column(z, p).reshape(8, 32, 128), 0, 1)
            out_ref[g, 32 * p:32 * (p + 1)] = moved
        out_copies[g].start()
    for copy in out_copies:
        copy.wait()


def prepare_middle_kernel(roster_ref, gates_ref, w_ref):
    gate = functools.partial(gate_at, gates_ref, roster_ref)
    w_ref[0:128, :384] = operand(gate(3), HC, HC)
    w_ref[128:256, :384] = operand(compose(gate(5), gate(4)), HCM, HCL)
    w_ref[256:384, :384] = operand(gate(6), HC, HC)
    w_ref[384:512, :384] = operand(gate(7), HC, HC)
    w_ref[512:] = lane_exchange()


def prepare_last_kernel(roster_ref, gates_ref, w_ref):
    gate = functools.partial(gate_at, gates_ref, roster_ref)
    w_ref[0:128, :384] = operand(compose(gate(8), gate(2)), HC, ROT)
    w_ref[128:256, :384] = operand(gate(9), HC, HCL)
    w_ref[256:] = lane_exchange()


def middle_kernel(w_ref, x_ref, out_ref, mid_ref, low_ref, high_ref):
    w3, wk, w6, w7 = [w_ref[128 * k:128 * (k + 1), :384] for k in range(4)]
    swap = w_ref[512:]
    for g in range(4):
        y = apply(w3, unpack(x_ref[:, 8 * g:8 * (g + 1), :]))
        moved = pack([column(y, j) for j in range(8)])
        mid_ref[:, :, 8 * g:8 * (g + 1), :] = moved.reshape(32, 4, 8, 128)
    contiguous(wk, mid_ref, low_ref)
    for q in range(4):
        y = apply(w6, unpack(low_ref[:, :, 8 * q:8 * (q + 1), :].reshape(128, 8, 128)))
        for j in range(8):
            high_ref[q, j] = column(y, j)
    for i in range(8):
        z = exchange_lanes(swap, columns([high_ref[q, i] for q in range(4)]))
        x = columns(
            [jnp.concatenate([column(z, p)[32 * j:32 * (j + 1)] for p in range(4)], 0) for j in range(4)]
        )
        y = apply(w7, x)
        for j in range(4):
            mid_ref[8 * j + i] = column(y, j).reshape(4, 32, 128)
    for j in range(4):
        moved = pack([mid_ref[8 * j + i].reshape(128, 128) for i in range(8)])
        out_ref[:, j] = moved.reshape(64, 2, 8, 128)


def last_kernel(w_ref, x_ref, out_hbm, mid_ref, high_ref, out_ref, sems):
    wh, w9 = w_ref[0:128, :384], w_ref[128:256, :384]
    swap = w_ref[256:]
    out_copies = [
        pltpu.make_async_copy(out_ref.at[4 * i:4 * i + 4], out_hbm.at[4 * i:4 * i + 4], sems.at[i])
        for i in range(8)
    ]
    for e in range(4):
        y = apply(wh, unpack(x_ref[e]))
        for j in range(8):
            high_ref[e, j] = column(y, j)
    for g in range(4):
        blocks = []
        for i in range(2):
            z = exchange_lanes(swap, columns([high_ref[e, 2 * g + i] for e in range(4)]))
            blocks += [column(z, p) for p in range(4)]
        mid_ref[:, :, 8 * g:8 * (g + 1), :] = pack(blocks).reshape(32, 4, 8, 128)
    contiguous(w9, mid_ref, out_ref, after=lambda i: out_copies[i].start())
    for copy in out_copies:
        copy.wait()


WHOLE = pl.BlockSpec(memory_space=pltpu.VMEM)
SCALARS = pl.BlockSpec(memory_space=pltpu.SMEM)
IN_HBM = pl.BlockSpec(memory_space=pltpu.HBM)
OPERANDS = [jax.ShapeDtypeStruct((rows, 512), BF16) for rows in (1024, 768)]
MID = pltpu.VMEM((32, 4, 32, 128), F32)
FLAT = pltpu.VMEM((32, 128, 128), F32)
HIGH = pltpu.VMEM((4, 8, 128, 128), F32)
PARAMS = pltpu.CompilerParams(vmem_limit_bytes=16 * 1024 * 1024)
ALL_VMEM = pltpu.CompilerParams(vmem_limit_bytes=63 * 1024 * 1024)


def amps_like(*shape):
    return jax.ShapeDtypeStruct(shape + (128,), F32)


def exchange(amps, axes):
    count = lax.axis_size(axes)
    chunks = amps.reshape(count, -1, 128)
    return lax.all_to_all(chunks, axes, split_axis=0, concat_axis=0, tiled=True)


def prepare(kernel, shape, roster, gates):
    return pl.pallas_call(
        kernel, out_shape=shape, in_specs=[SCALARS, WHOLE], out_specs=WHOLE, compiler_params=PARAMS,
        name="prepare",
    )(roster, gates)


def on_device(state, gates, roster):
    rows = state.reshape(2, -1, 128).swapaxes(0, 1).reshape(32, 128, 128)
    amps = pl.pallas_call(
        first_kernel, out_shape=amps_like(128, 32), in_specs=[IN_HBM] * 3, out_specs=IN_HBM,
        scratch_shapes=[
            pltpu.SMEM(roster.shape, roster.dtype), pltpu.VMEM(gates.shape, gates.dtype), FLAT, MID,
            pltpu.VMEM((4, 128, 8, 128), F32), pltpu.SemaphoreType.DMA((14,)),
        ],
        compiler_params=ALL_VMEM, name="first",
    )(roster, gates, rows)
    for_middle = prepare(prepare_middle_kernel, OPERANDS[0], roster, gates)
    amps = exchange(amps, ("wide",)).reshape(128, 32, 128)
    amps = pl.pallas_call(
        middle_kernel, out_shape=amps_like(64, 4, 2, 8), in_specs=[WHOLE] * 2, out_specs=WHOLE,
        scratch_shapes=[MID, MID, HIGH], compiler_params=PARAMS, name="middle",
    )(for_middle, amps)
    amps, later = lax.optimization_barrier((amps, roster))
    for_last = prepare(prepare_last_kernel, OPERANDS[1], later, gates)
    amps = exchange(amps, ("wide", "narrow")).reshape(4, 128, 8, 128)
    amps = pl.pallas_call(
        last_kernel, out_shape=amps_like(32, 128), in_specs=[WHOLE] * 2, out_specs=IN_HBM,
        scratch_shapes=[MID, HIGH, FLAT, pltpu.SemaphoreType.DMA((8,))], compiler_params=PARAMS, name="last",
    )(for_last, amps)
    return amps.reshape(-1, 2, 128).swapaxes(0, 1).reshape(2, -1)


def solution(mesh):
    in_specs = (P(None, ("wide", "narrow")), P(), P())
    out_specs = P(None, ("wide", "narrow"))
    return jax.shard_map(
        on_device, mesh=mesh, in_specs=in_specs, out_specs=out_specs, check_vma=False
    )
```
